512 devices in a mesh: row: 16 (over z, core), col: 32 (over x, y).
Axes of the slice: x: 4, y: 8, z: 8, core: 2. Of those that a mesh axis runs over, the one named last changes fastest.
Arguments:
- graph_emb: float32 [16384, 256], P('row', 'col'), may hold values from -40 to 40
- conf_emb: float32 [16384, 256], P('col', 'row'), may hold values from -40 to 40
Outputs:
- grad_graph: float32 [16384, 256], P('row', 'col')
- grad_conf: float32 [16384, 256], P('col', 'row')
- row_potential: float32 [16384], P('row')
- col_potential: float32 [16384], P('col')
The draws below stay inside these ranges and needn't reach their ends.
All inputs are finite; a program needn't handle non-finite values.
Results may differ from the reference program's by a relative error of at most 0.0003.
Values sent between devices are 32-bit elements; how exact they have to be, the bound alone decides.
No kernel may reach another device: no remote copies, remote signals or barrier semaphores. Data moves between devices by JAX's collectives and lax.ppermute only.
A program may use at most 64 MiB of HBM per device.

```python
import math
import jax
import jax.numpy as jnp
from jax import lax

EMBED = 256
ROWS_DEV = 1024
ITERS = 3
BATCH = 16384


def joint_pair(key):
    base = jax.random.normal(jax.random.fold_in(key, 11), (BATCH, EMBED), jnp.float32)
    row_scale = jnp.exp(jax.random.uniform(jax.random.fold_in(key, 12), (BATCH, 1), jnp.float32, -0.5, 0.5))
    noise = jax.random.normal(jax.random.fold_in(key, 13), (BATCH, EMBED), jnp.float32)
    common = jnp.where(jax.random.uniform(jax.random.fold_in(key, 19), (EMBED,), jnp.float32) < 0.5, -1.0, 1.0).astype(jnp.float32)
    graph_view = base * row_scale + common[None, :]
    conf_view = 0.6 * graph_view + 0.8 * noise
    pair_signs = jnp.where(jax.random.uniform(jax.random.fold_in(key, 15), (BATCH, EMBED // 2), jnp.float32) < 0.5, -1.0, 1.0).astype(jnp.float32)
    alternate = jnp.stack([pair_signs, -pair_signs], axis=2).reshape(BATCH, EMBED)
    level = jax.random.randint(jax.random.fold_in(key, 16), (BATCH, 1), 0, 4).astype(jnp.float32)
    strength = 120.0 + 60.0 * level
    amplitude = jnp.sqrt(strength * EMBED ** (-0.5))
    aligned = amplitude * alternate * common[None, :] + common[None, :]
    index = jnp.arange(BATCH)[:, None]
    first = index % 32 == 0
    second = index % 32 == 1
    repelled = index % 512 == 7
    prior_aligned = jnp.roll(aligned, 1, axis=0)
    prior_strength = jnp.roll(strength, 1, axis=0)
    extra = jax.random.normal(jax.random.fold_in(key, 17), (BATCH, EMBED), jnp.float32)
    near_copy = prior_aligned * (1.0 - 2.0 / prior_strength) + 0.3 * extra
    outlier = -24.0 * common[None, :] + 2.0 * noise
    graph_view = jnp.where(first, aligned, graph_view)
    conf_view = jnp.where(first, aligned, jnp.where(second, near_copy, conf_view))
    conf_view = jnp.where(repelled, outlier, conf_view)
    graph_view = jnp.clip(graph_view, -40.0, 40.0)
    conf_view = jnp.clip(conf_view, -40.0, 40.0)
    order = jax.random.permutation(jax.random.fold_in(key, 18), BATCH)
    return (graph_view[order], conf_view[order])


def draw_graph_emb(key, part):
    return joint_pair(key)[0]


def draw_conf_emb(key, part):
    return joint_pair(key)[1]


def setup_inputs(seed: int = 0) -> dict:
    key_list = jax.random.split(jax.random.key(seed), 3)
    graph_emb = draw_graph_emb(jax.random.fold_in(key_list[2], 71), 0)
    conf_emb = draw_conf_emb(jax.random.fold_in(key_list[2], 71), 0)
    return {"graph_emb": graph_emb, "conf_emb": conf_emb}


entropy_weight = 1.0


def cost_block(graph_part, conf_all):
    products = lax.dot_general(graph_part, conf_all, (((1,), (1,)), ((), ())), precision=lax.Precision.HIGHEST, preferred_element_type=jnp.float32)
    return -products * (EMBED ** -0.5)


def reference(graph_emb, conf_emb):
    block_count = BATCH // ROWS_DEV
    graph_blocks = graph_emb.reshape(block_count, ROWS_DEV, EMBED)
    log_weight = -math.log(BATCH)
    row_pot = jnp.zeros((BATCH,), jnp.float32)
    col_pot = jnp.zeros((BATCH,), jnp.float32)
    for sweep_index in range(ITERS):
        def row_pass(graph_part):
            scores = (col_pot[None, :] - cost_block(graph_part, conf_emb)) / entropy_weight
            peak_value = jnp.max(scores, axis=1)
            return peak_value + jnp.log(jnp.sum(jnp.exp(scores - peak_value[:, None]), axis=1))
        row_lse = lax.map(row_pass, graph_blocks).reshape(BATCH)
        row_pot = entropy_weight * (log_weight - row_lse)
        pot_blocks = row_pot.reshape(block_count, ROWS_DEV)

        def col_step(carry, items):
            running_max, running_sum = carry
            graph_part, pot_part = items
            scores = (pot_part[:, None] - cost_block(graph_part, conf_emb)) / entropy_weight
            new_max = jnp.maximum(running_max, jnp.max(scores, axis=0))
            new_sum = running_sum * jnp.exp(running_max - new_max) + jnp.sum(jnp.exp(scores - new_max[None, :]), axis=0)
            return (new_max, new_sum), None

        start_max = jnp.full((BATCH,), -jnp.inf, jnp.float32)
        start_sum = jnp.zeros((BATCH,), jnp.float32)
        (final_max, final_sum), unused = lax.scan(col_step, (start_max, start_sum), (graph_blocks, pot_blocks))
        col_pot = entropy_weight * (log_weight - (final_max + jnp.log(final_sum)))
    factor = -BATCH * (EMBED ** -0.5)
    pot_blocks = row_pot.reshape(block_count, ROWS_DEV)

    def grad_step(conf_total, items):
        graph_part, pot_part = items
        transport = jnp.exp((pot_part[:, None] + col_pot[None, :] - cost_block(graph_part, conf_emb)) / entropy_weight)
        graph_grad = jnp.dot(transport, conf_emb, precision=lax.Precision.HIGHEST, preferred_element_type=jnp.float32)
        conf_part = lax.dot_general(transport, graph_part, (((0,), (0,)), ((), ())), precision=lax.Precision.HIGHEST, preferred_element_type=jnp.float32)
        return conf_total + conf_part, graph_grad

    conf_total, graph_grads = lax.scan(grad_step, jnp.zeros((BATCH, EMBED), jnp.float32), (graph_blocks, pot_blocks))
    grad_graph = graph_grads.reshape(BATCH, EMBED) * factor
    grad_conf = conf_total * factor
    return (grad_graph, grad_conf, row_pot, col_pot)
```

```python
import math

import jax
import jax.numpy as jnp
from jax import lax
from jax.sharding import PartitionSpec as P

ITERS = 3
LANES = 128


def spread(block, axis):
    n = lax.axis_size(axis)
    return lax.all_to_all(jnp.broadcast_to(block[None], (n,) + block.shape), axis, 0, 0)


def swap(chunks, axis):
    return lax.all_to_all(chunks, axis, 0, 0)


def lse(values, dim):
    peak = jnp.max(values, axis=dim, keepdims=True)
    total = jnp.sum(jnp.exp(values - peak), axis=dim)
    return jnp.squeeze(peak, dim) + jnp.log(total)


def shared_lse(partial, axis):
    parts = spread(partial.reshape(-1, LANES), axis)
    return lse(parts, 0).reshape(partial.shape)


def per_device(graph_emb, conf_emb):
    graph_part, conf_part = graph_emb.T, conf_emb.T
    conf_t = spread(conf_part, "row").reshape(-1, conf_part.shape[1])
    graph_t = spread(graph_part, "col").reshape(-1, graph_part.shape[1])
    width, rows = graph_t.shape
    cols = conf_t.shape[1]
    batch = rows * lax.axis_size("row")
    scale = width ** (-0.5)
    score = (
        lax.dot_general(
            graph_t,
            conf_t,
            (((0,), (0,)), ((), ())),
            precision=lax.Precision.HIGHEST,
            preferred_element_type=jnp.float32,
        )
        * scale
    )
    log_weight = -math.log(batch)
    row_pot = jnp.zeros((rows,), jnp.float32)
    col_pot = jnp.zeros((cols,), jnp.float32)
    for _ in range(ITERS):
        row_pot = log_weight - shared_lse(lse(col_pot[None, :] + score, 1), "col")
        col_pot = log_weight - shared_lse(lse(row_pot[:, None] + score, 0), "row")
    plan = jnp.exp(row_pot[:, None] + col_pot[None, :] + score)
    factor = -batch * scale
    conf_term = (
        lax.dot_general(
            graph_t,
            plan,
            (((1,), (0,)), ((), ())),
            precision=lax.Precision.HIGHEST,
            preferred_element_type=jnp.float32,
        )
        * factor
    )
    graph_term = (
        lax.dot_general(
            conf_t,
            plan,
            (((1,), (1,)), ((), ())),
            precision=lax.Precision.HIGHEST,
            preferred_element_type=jnp.float32,
        )
        * factor
    )
    conf_parts = swap(conf_term.reshape(lax.axis_size("row"), -1, cols), "row")
    graph_parts = swap(graph_term.reshape(lax.axis_size("col"), -1, rows), "col")
    grad_conf = jnp.sum(conf_parts, axis=0).T
    grad_graph = jnp.sum(graph_parts, axis=0).T
    return (grad_graph, grad_conf, row_pot, col_pot)


def solution(mesh):
    return jax.shard_map(
        per_device,
        mesh=mesh,
        in_specs=(P("row", "col"), P("col", "row")),
        out_specs=(P("row", "col"), P("col", "row"), P("row"), P("col")),
        check_vma=False,
    )
```

```python
import math

import jax
import jax.numpy as jnp
from jax import lax
from jax.sharding import PartitionSpec as P


ITERS = 3
LANES = 128


def spread(block, axis):
    n = lax.axis_size(axis)
    return lax.all_to_all(jnp.broadcast_to(block[None], (n,) + block.shape), axis, 0, 0)


def swap(chunks, axis):
    return lax.all_to_all(chunks, axis, 0, 0)


def fold(chunks, axis):
    me = lax.axis_index(axis).astype(jnp.uint32)
    n = chunks.shape[0]
    step = 1
    while n > 1:
        pairs = chunks.reshape((n // 2, 2) + chunks.shape[1:])
        bit = (me >> (step.bit_length() - 1)) & 1
        mine = lax.dynamic_index_in_dim(pairs, bit, 1, keepdims=False)
        other = lax.dynamic_index_in_dim(pairs, 1 - bit, 1, keepdims=False)
        partner = [(k, k ^ step) for k in range(lax.axis_size(axis))]
        chunks = mine + lax.ppermute(other, axis, partner)
        n, step = n // 2, step * 2
    return chunks[0]


def lse(values, dim):
    peak = jnp.max(values, axis=dim, keepdims=True)
    total = jnp.sum(jnp.exp(values - peak), axis=dim)
    return jnp.squeeze(peak, dim) + jnp.log(total)


def shared_lse(partial, axis):
    parts = spread(partial.reshape(-1, LANES), axis)
    return lse(parts, 0).reshape(partial.shape)


def gather_parts(graph_part, conf_part):
    graph_t = spread(graph_part, "col")
    conf_t = lax.all_gather(conf_part, "row")
    return graph_t.reshape(-1, graph_part.shape[1]), conf_t.reshape(-1, conf_part.shape[1])


def matmul(lhs, rhs, contract):
    return lax.dot_general(
        lhs,
        rhs,
        (contract, ((), ())),
        precision=lax.Precision.HIGHEST,
        preferred_element_type=jnp.float32,
    )


def steps(graph_emb, conf_emb):
    graph_t, conf_t = gather_parts(graph_emb.T, conf_emb.T)
    width, rows = graph_t.shape
    cols = conf_t.shape[1]
    batch = rows * lax.axis_size("row")
    scale = width ** (-0.5)
    score = matmul(graph_t, conf_t, ((0,), (0,))) * scale
    log_weight = -math.log(batch)
    row_pot = jnp.zeros((rows,), jnp.float32)
    col_pot = jnp.zeros((cols,), jnp.float32)
    for _ in range(ITERS):
        row_pot = log_weight - shared_lse(lse(col_pot[None, :] + score, 1), "col")
        col_pot = log_weight - shared_lse(lse(row_pot[:, None] + score, 0), "row")
    plan = jnp.exp(row_pot[:, None] + col_pot[None, :] + score)
    factor = -batch * scale
    graph_term = matmul(conf_t, plan, ((1,), (1,))) * factor
    graph_parts = swap(graph_term.reshape(lax.axis_size("col"), -1, rows), "col")
    conf_term = matmul(graph_t, plan, ((1,), (0,))) * factor
    grad_conf = fold(conf_term.reshape(lax.axis_size("row"), -1, cols), "row").T
    grad_graph = jnp.sum(graph_parts, axis=0).T
    return (grad_graph, grad_conf, row_pot, col_pot)


def solution(mesh):
    return jax.shard_map(
        steps,
        mesh=mesh,
        in_specs=(P("row", "col"), P("col", "row")),
        out_specs=(P("row", "col"), P("col", "row"), P("row"), P("col")),
        check_vma=False,
    )
```

```python
import math

import jax
import jax.numpy as jnp
from jax import lax
from jax.sharding import PartitionSpec as P


ITERS = 3
LANES = 128


def spread(block, axis):
    n = lax.axis_size(axis)
    return lax.all_to_all(jnp.broadcast_to(block[None], (n,) + block.shape), axis, 0, 0)


def swap(chunks, axis):
    return lax.all_to_all(chunks, axis, 0, 0)


def fold(chunks, axis):
    me = lax.axis_index(axis).astype(jnp.uint32)
    n, shift = chunks.shape[0], 0
    while n > 1:
        radix = n if n <= 4 else 2
        groups = chunks.reshape((n // radix, radix) + chunks.shape[1:])
        digit = (me >> shift) & (radix - 1)
        chunks = lax.dynamic_index_in_dim(groups, digit, 1, keepdims=False)
        for d in range(1, radix):
            sent = lax.dynamic_index_in_dim(groups, digit ^ d, 1, keepdims=False)
            partner = [(k, k ^ (d << shift)) for k in range(lax.axis_size(axis))]
            chunks = chunks + lax.ppermute(sent, axis, partner)
        n, shift = n // radix, shift + radix.bit_length() - 1
    return chunks[0]


def lse(values, dim):
    peak = jnp.max(values, axis=dim, keepdims=True)
    total = jnp.sum(jnp.exp(values - peak), axis=dim)
    return jnp.squeeze(peak, dim) + jnp.log(total)


def shared_lse(partial, axis):
    parts = spread(partial.reshape(-1, LANES), axis)
    return lse(parts, 0).reshape(partial.shape)


def gather_parts(graph_part, conf_part):
    graph_t = spread(graph_part, "col")
    conf_t = lax.all_gather(conf_part, "row")
    return graph_t.reshape(-1, graph_part.shape[1]), conf_t.reshape(-1, conf_part.shape[1])


def matmul(lhs, rhs, contract, precision):
    return lax.dot_general(
        lhs,
        rhs,
        (contract, ((), ())),
        precision=precision,
        preferred_element_type=jnp.float32,
    )


def steps(graph_emb, conf_emb):
    graph_t, conf_t = gather_parts(graph_emb.T, conf_emb.T)
    width, rows = graph_t.shape
    cols = conf_t.shape[1]
    batch = rows * lax.axis_size("row")
    scale = width ** (-0.5)
    score = matmul(graph_t, conf_t, ((0,), (0,)), lax.Precision.HIGHEST) * scale
    log_weight = -math.log(batch)
    row_pot = jnp.zeros((rows,), jnp.float32)
    col_pot = jnp.zeros((cols,), jnp.float32)
    for _ in range(ITERS):
        row_pot = log_weight - shared_lse(lse(col_pot[None, :] + score, 1), "col")
        col_pot = log_weight - shared_lse(lse(row_pot[:, None] + score, 0), "row")
    plan = jnp.exp(row_pot[:, None] + col_pot[None, :] + score)
    factor = -batch * scale
    graph_term = matmul(conf_t, plan, ((1,), (1,)), lax.Precision.HIGH) * factor
    graph_parts = swap(graph_term.reshape(lax.axis_size("col"), -1, rows), "col")
    conf_term = matmul(graph_t, plan, ((1,), (0,)), lax.Precision.HIGH) * factor
    grad_conf = fold(conf_term.reshape(lax.axis_size("row"), -1, cols), "row").T
    grad_graph = jnp.sum(graph_parts, axis=0).T
    return (grad_graph, grad_conf, row_pot, col_pot)


def solution(mesh):
    return jax.shard_map(
        steps,
        mesh=mesh,
        in_specs=(P("row", "col"), P("col", "row")),
        out_specs=(P("row", "col"), P("col", "row"), P("row"), P("col")),
        check_vma=False,
    )
```

```python
import math

import jax
import jax.numpy as jnp
from jax import lax
from jax.sharding import PartitionSpec as P


ITERS = 3
LANES = 128


def spread(block, axis):
    n = lax.axis_size(axis)
    return lax.all_to_all(jnp.broadcast_to(block[None], (n,) + block.shape), axis, 0, 0)


def swap(chunks, axis):
    return lax.all_to_all(chunks, axis, 0, 0)


def fold(groups, dim, axis, shift):
    size = groups.shape[dim]
    digit = (lax.axis_index(axis).astype(jnp.uint32) >> shift) & (size - 1)
    total = lax.dynamic_index_in_dim(groups, digit, dim, keepdims=False)
    for d in range(1, size):
        sent = lax.dynamic_index_in_dim(groups, digit ^ d, dim, keepdims=False)
        partner = [(k, k ^ (d << shift)) for k in range(lax.axis_size(axis))]
        total = total + lax.ppermute(sent, axis, partner)
    return total


def lse(values, dim):
    peak = jnp.max(values, axis=dim, keepdims=True)
    total = jnp.sum(jnp.exp(values - peak), axis=dim)
    return jnp.squeeze(peak, dim) + jnp.log(total)


def shared_lse(partial, axis):
    parts = spread(partial.reshape(-1, LANES), axis)
    return lse(parts, 0).reshape(partial.shape)


def gather_parts(graph_part, conf_part):
    graph_t = spread(graph_part, "col")
    conf_t = lax.all_gather(conf_part, "row")
    return graph_t.reshape(-1, graph_part.shape[1]), conf_t.reshape(-1, conf_part.shape[1])


def matmul(lhs, rhs, contract, precision):
    return lax.dot_general(
        lhs,
        rhs,
        (contract, ((), ())),
        precision=precision,
        preferred_element_type=jnp.float32,
    )


def steps(graph_emb, conf_emb):
    graph_t, conf_t = gather_parts(graph_emb.T, conf_emb.T)
    width, rows = graph_t.shape
    cols = conf_t.shape[1]
    batch = rows * lax.axis_size("row")
    scale = width ** (-0.5)
    score = matmul(graph_t, conf_t, ((0,), (0,)), lax.Precision.HIGHEST) * scale
    log_weight = -math.log(batch)
    row_pot = jnp.zeros((rows,), jnp.float32)
    col_pot = jnp.zeros((cols,), jnp.float32)
    for _ in range(ITERS):
        row_pot = log_weight - shared_lse(lse(col_pot[None, :] + score, 1), "col")
        col_pot = log_weight - shared_lse(lse(row_pot[:, None] + score, 0), "row")
    plan = jnp.exp(row_pot[:, None] + col_pot[None, :] + score)
    factor = -batch * scale
    conf_term = matmul(graph_t, plan, ((1,), (0,)), lax.Precision.HIGH) * factor
    digits = conf_term.reshape(lax.axis_size("row") // 4, 2, 2, -1, cols)
    digits = fold(digits, 1, "row", 1)
    graph_term = matmul(conf_t, plan, ((1,), (1,)), lax.Precision.HIGH) * factor
    graph_parts = swap(graph_term.reshape(lax.axis_size("col"), -1, rows), "col")
    digits = fold(digits, 1, "row", 0)
    grad_conf = fold(digits, 0, "row", 2).T
    grad_graph = jnp.sum(graph_parts, axis=0).T
    return (grad_graph, grad_conf, row_pot, col_pot)


def solution(mesh):
    return jax.shard_map(
        steps,
        mesh=mesh,
        in_specs=(P("row", "col"), P("col", "row")),
        out_specs=(P("row", "col"), P("col", "row"), P("row"), P("col")),
        check_vma=False,
    )
```

```python
import math

import jax
import jax.numpy as jnp
from jax import lax
from jax.sharding import PartitionSpec as P


ITERS = 3
LANES = 128


def spread(block, axis):
    n = lax.axis_size(axis)
    return lax.all_to_all(jnp.broadcast_to(block[None], (n,) + block.shape), axis, 0, 0)


def swap(chunks, axis):
    return lax.all_to_all(chunks, axis, 0, 0)


def fold(chunks, axis):
    me = lax.axis_index(axis).astype(jnp.uint32)
    n, shift = chunks.shape[0], 0
    while n > 1:
        radix = n if n <= 4 else 2
        groups = chunks.reshape((n // radix, radix) + chunks.shape[1:])
        digit = (me >> shift) & (radix - 1)
        chunks = lax.dynamic_index_in_dim(groups, digit, 1, keepdims=False)
        for d in range(1, radix):
            sent = lax.dynamic_index_in_dim(groups, digit ^ d, 1, keepdims=False)
            partner = [(k, k ^ (d << shift)) for k in range(lax.axis_size(axis))]
            chunks = chunks + lax.ppermute(sent, axis, partner)
        n, shift = n // radix, shift + radix.bit_length() - 1
    return chunks[0]


def local_lse(values, dim):
    peak = jnp.max(values, axis=dim, keepdims=True)
    mass = jnp.exp(values - peak)
    peak = jnp.squeeze(peak, dim)
    return peak + jnp.log(jnp.sum(mass, axis=dim)), peak, mass


def shared_lse(partial, axis):
    parts = spread(partial.reshape(-1, LANES), axis)
    return local_lse(parts, 0)[0].reshape(partial.shape)


def gather_parts(graph_part, conf_part):
    graph_t = spread(graph_part, "col")
    conf_t = lax.all_gather(conf_part, "row")
    return graph_t.reshape(-1, graph_part.shape[1]), conf_t.reshape(-1, conf_part.shape[1])


def matmul(lhs, rhs, contract, precision):
    return lax.dot_general(
        lhs,
        rhs,
        (contract, ((), ())),
        precision=precision,
        preferred_element_type=jnp.float32,
    )


def steps(graph_emb, conf_emb):
    graph_t, conf_t = gather_parts(graph_emb.T, conf_emb.T)
    width, rows = graph_t.shape
    cols = conf_t.shape[1]
    batch = rows * lax.axis_size("row")
    scale = width ** (-0.5)
    score = matmul(graph_t, conf_t, ((0,), (0,)), lax.Precision.HIGHEST) * scale
    log_weight = -math.log(batch)
    row_pot = jnp.zeros((rows,), jnp.float32)
    col_pot = jnp.zeros((cols,), jnp.float32)
    for _ in range(ITERS):
        partial, _, _ = local_lse(col_pot[None, :] + score, 1)
        row_pot = log_weight - shared_lse(partial, "col")
        partial, col_peak, mass = local_lse(row_pot[:, None] + score, 0)
        col_pot = log_weight - shared_lse(partial, "row")
    factor = -batch * scale
    conf_mass = matmul(graph_t, mass, ((1,), (0,)), lax.Precision.HIGH)
    conf_mass = lax.optimization_barrier(conf_mass)
    col_scale = factor * jnp.exp(col_peak + col_pot)
    plan = jnp.exp(row_pot[:, None] + col_pot[None, :] + score)
    graph_term = matmul(conf_t, plan, ((1,), (1,)), lax.Precision.HIGH) * factor
    graph_parts = swap(graph_term.reshape(lax.axis_size("col"), -1, rows), "col")
    conf_term = conf_mass * col_scale
    grad_conf = fold(conf_term.reshape(lax.axis_size("row"), -1, cols), "row").T
    grad_graph = jnp.sum(graph_parts, axis=0).T
    return (grad_graph, grad_conf, row_pot, col_pot)


def solution(mesh):
    return jax.shard_map(
        steps,
        mesh=mesh,
        in_specs=(P("row", "col"), P("col", "row")),
        out_specs=(P("row", "col"), P("col", "row"), P("row"), P("col")),
        check_vma=False,
    )
```

```python
import math

import jax
import jax.numpy as jnp
from jax import lax
from jax.sharding import PartitionSpec as P


ITERS = 3
LANES = 128
Y_CHIPS = 8


def spread(block, axis, groups=None):
    n = lax.axis_size(axis) if groups is None else len(groups[0])
    copies = jnp.broadcast_to(block[None], (n,) + block.shape)
    return lax.all_to_all(copies, axis, 0, 0, axis_index_groups=groups)


def swap(chunks, axis):
    return lax.all_to_all(chunks, axis, 0, 0)


def fold(chunks, axis):
    me = lax.axis_index(axis).astype(jnp.uint32)
    n, shift = chunks.shape[0], 0
    while n > 1:
        radix = n if n <= 4 else 2
        groups = chunks.reshape((n // radix, radix) + chunks.shape[1:])
        digit = (me >> shift) & (radix - 1)
        chunks = lax.dynamic_index_in_dim(groups, digit, 1, keepdims=False)
        for d in range(1, radix):
            sent = lax.dynamic_index_in_dim(groups, digit ^ d, 1, keepdims=False)
            partner = [(k, k ^ (d << shift)) for k in range(lax.axis_size(axis))]
            chunks = chunks + lax.ppermute(sent, axis, partner)
        n, shift = n // radix, shift + radix.bit_length() - 1
    return chunks[0]


def local_lse(values, dim):
    peak = jnp.max(values, axis=dim, keepdims=True)
    mass = jnp.exp(values - peak)
    peak = jnp.squeeze(peak, dim)
    return peak + jnp.log(jnp.sum(mass, axis=dim)), peak, mass


def shared_lse(partial, axis):
    parts = spread(partial.reshape(-1, LANES), axis)
    return local_lse(parts, 0)[0].reshape(partial.shape)


def gather_parts(graph_part, conf_part):
    x_chips = lax.axis_size("col") // Y_CHIPS
    same_x = [[x * Y_CHIPS + y for y in range(Y_CHIPS)] for x in range(x_chips)]
    same_y = [[x * Y_CHIPS + y for x in range(x_chips)] for y in range(Y_CHIPS)]
    along_y = spread(graph_part, "col", same_x)
    graph_t = spread(along_y, "col", same_y)
    conf_t = lax.all_gather(conf_part, "row")
    return graph_t.reshape(-1, graph_part.shape[1]), conf_t.reshape(-1, conf_part.shape[1])


def matmul(lhs, rhs, contract, precision):
    return lax.dot_general(
        lhs,
        rhs,
        (contract, ((), ())),
        precision=precision,
        preferred_element_type=jnp.float32,
    )


def steps(graph_emb, conf_emb):
    graph_t, conf_t = gather_parts(graph_emb.T, conf_emb.T)
    width, rows = graph_t.shape
    cols = conf_t.shape[1]
    batch = rows * lax.axis_size("row")
    scale = width ** (-0.5)
    score = matmul(graph_t, conf_t, ((0,), (0,)), lax.Precision.HIGHEST) * scale
    log_weight = -math.log(batch)
    row_pot = jnp.zeros((rows,), jnp.float32)
    col_pot = jnp.zeros((cols,), jnp.float32)
    for _ in range(ITERS):
        partial, _, _ = local_lse(col_pot[None, :] + score, 1)
        row_pot = log_weight - shared_lse(partial, "col")
        partial, col_peak, mass = local_lse(row_pot[:, None] + score, 0)
        col_pot = log_weight - shared_lse(partial, "row")
    factor = -batch * scale
    conf_mass = matmul(graph_t, mass, ((1,), (0,)), lax.Precision.HIGH)
    conf_mass = lax.optimization_barrier(conf_mass)
    col_scale = factor * jnp.exp(col_peak + col_pot)
    plan = jnp.exp(row_pot[:, None] + col_pot[None, :] + score)
    graph_term = matmul(conf_t, plan, ((1,), (1,)), lax.Precision.HIGH) * factor
    graph_parts = swap(graph_term.reshape(lax.axis_size("col"), -1, rows), "col")
    conf_term = conf_mass * col_scale
    grad_conf = fold(conf_term.reshape(lax.axis_size("row"), -1, cols), "row").T
    grad_graph = jnp.sum(graph_parts, axis=0).T
    return (grad_graph, grad_conf, row_pot, col_pot)


def solution(mesh):
    return jax.shard_map(
        steps,
        mesh=mesh,
        in_specs=(P("row", "col"), P("col", "row")),
        out_specs=(P("row", "col"), P("col", "row"), P("row"), P("col")),
        check_vma=False,
    )
```
